32 devices in a mesh: dp: 2 (over x), context: 16 (over z, y, core).
Axes of the slice: x: 2, y: 2, z: 4, core: 2. Of those that a mesh axis runs over, the one named last changes fastest.
Arguments:
- grad_out: bfloat16 [2, 2048, 4096], P('dp', 'context'), may hold values from -6 to 6
- attn: bfloat16 [2, 2048, 4096], P('dp', 'context'), may hold values from -0.09375 to 0.09375
- w_out: bfloat16 [4096, 4096], P('context'), may hold values from -0.09375 to 0.09375
Outputs:
- grad_attn: bfloat16 [2, 2048, 4096], P('dp', None, 'context')
- grad_w: bfloat16 [4096, 4096], P('context')
The draws below stay inside these ranges and needn't reach their ends.
All inputs are finite; a program needn't handle non-finite values.
Results may differ from the reference program's by a relative error of at most 0.013.
Values may be sent and summed in bfloat16 or wider, within the bound.
A program may use at most 128 MiB of HBM per device.

```python
import jax
import jax.numpy as jnp
from jax import lax

D = 4096
HD = 4096
LEN = 2048
SEQS = 2


def shard_levels(key, shape, split, smallest, top_value):
    loudness, own = 1.0, jax.random.fold_in(key, 6)
    for dim, parts in split:
        heights = jnp.exp(jax.random.uniform(jax.random.fold_in(own, dim), (parts,), jnp.float32, smallest / len(split), top_value / len(split)))
        loudness = loudness * jnp.repeat(heights, shape[dim] // parts).reshape([-1 if axis == dim else 1 for axis in range(len(shape))])
    return loudness


def scatter_about(stream_key, shape, width, reach, split=(), kind=jnp.bfloat16):
    entries = width * jax.random.normal(stream_key, shape, jnp.float32)
    if split:
        entries = entries * shard_levels(stream_key, shape, split, -0.22, 0.18)
    return jnp.clip(entries, -reach, reach).astype(kind)


def setup_inputs(seed: int = 0) -> dict:
    seeds = jax.random.split(jax.random.key(seed), 4)
    grad_out = scatter_about(seeds[0], (SEQS, LEN, D), 1.0, 6.0, ((0, 2), (1, 16)))
    attn = scatter_about(seeds[1], (SEQS, LEN, HD), ((SEQS * LEN) ** -0.5), 0.09375, ((0, 2), (1, 16)))
    w_out = scatter_about(seeds[2], (HD, D), HD ** -0.5, 0.09375, ((0, 16),))
    return {"grad_out": grad_out, "attn": attn, "w_out": w_out}


def reference(grad_out, attn, w_out):
    def one_sequence(totals, inputs):
        cotangent, activations = inputs
        head_grad = jnp.dot(cotangent, w_out.T, preferred_element_type=jnp.float32).astype(jnp.bfloat16)
        partial_grad = jnp.dot(activations.T, cotangent, preferred_element_type=jnp.float32).astype(jnp.bfloat16)
        partial_grad = lax.optimization_barrier(partial_grad)
        return totals + partial_grad.astype(jnp.float32), head_grad

    start_totals = jnp.zeros((w_out.shape[0], w_out.shape[1]), jnp.float32)
    totals, head_grads = lax.scan(one_sequence, start_totals, (grad_out, attn))
    return head_grads, totals.astype(jnp.bfloat16)
```

```python
import functools

import jax
import jax.numpy as jnp
from jax import lax
from jax.experimental import pallas as pl
from jax.experimental.pallas import tpu as pltpu
from jax.sharding import PartitionSpec as P

CHUNKS = 16
AHEAD = 2
AHEAD_Y = 12
CORES = 2
SIDE = 4
HOP = 1
PLANE = 1
MESH = pl.DeviceIdType.MESH


def grid_of(chips):
    fast = 1
    while (2 * fast) * (2 * fast) <= chips:
        fast *= 2
    return chips // fast, fast


def side_rows(tokens):
    return tokens * SIDE // 16


def kernel(dp, n, chunks, g_in, a_in, w_in, o_attn, o_w, gath, acts, acts_t, w, acc, part,
           z_send, z_recv, p_recv, ys_send, y_recv, f_recv, s_recv, a_send, a_recv, x_send, x_recv,
           own_sem, w_sem, own_a_sem):
    A, B = grid_of(n // CORES)
    tokens, width = g_in.shape
    heads = w_in.shape[0]
    F = width // chunks
    side = side_rows(tokens)
    line = A * tokens
    half = B * line
    me = lax.axis_index("context")
    rep = lax.axis_index("dp")
    c = lax.rem(me, CORES)
    b = lax.rem(me // CORES, B)
    a = me // (CORES * B)

    def ctx(a_, b_, c_):
        return (a_ * B + b_) * CORES + c_

    def others(i, size):
        return [lax.rem(i + d, size) for d in range(1, size)]

    def slot(i, t):
        s, bit = 0, 1
        while bit < A:
            s = s + bit * lax.rem(i // bit + t // bit, 2)
            bit *= 2
        return s

    pair = a + 1 - 2 * lax.rem(a, 2)

    def cols(k):
        return pl.ds(pl.multiple_of(k * F, F), F)

    def place(c_, u, s):
        return ((c_ * B + u) * A + s) * tokens

    def rows(k, lo, size):
        return gath.at[k, pl.ds(pl.multiple_of(lo, 16), size)]

    def own(k):
        return g_in.at[:, cols(k)]

    def remote(src, dst, send, recv, target):
        return pltpu.make_async_remote_copy(
            src_ref=src, dst_ref=dst, send_sem=send, recv_sem=recv, device_id=target, device_id_type=MESH)

    def inside(t):
        return jnp.logical_and(t >= 0, t < A)

    def own_copy(k):
        return pltpu.make_async_copy(own(k), rows(k, place(c, b, 0), tokens), own_sem.at[k])

    w_copy = pltpu.make_async_copy(w_in, w, w_sem)

    def head_cols(j):
        return pl.ds(pl.multiple_of(j * heads, heads), heads)

    own_act = pltpu.make_async_copy(a_in.at[:, head_cols(me)], acts.at[(c * B + b) * A], own_a_sem)

    own_act.start()
    w_copy.start()

    @pl.loop(0, chunks)
    def _(k):
        own_copy(k).start()

    barrier = pltpu.get_barrier_semaphore()
    for j in others(me, n):
        pl.semaphore_signal(barrier, inc=1, device_id={"context": j}, device_id_type=MESH)
    for r in others(rep, dp):
        pl.semaphore_signal(barrier, inc=1, device_id={"dp": r}, device_id_type=MESH)
    pl.semaphore_wait(barrier, n - 1 + dp - 1)

    def z_move(src, k, t, target):
        s = slot(target, t)
        return remote(src, rows(k, place(c, b, s), tokens), z_send.at[k], z_recv.at[k, s],
                      {"context": ctx(target, b, c)})

    def z_own(k):
        for sign in (1, -1):
            @pl.when(inside(a + sign))
            def _():
                z_move(own(k), k, a, a + sign).start()

    def y_own(k):
        for u in others(b, B):
            remote(own(k), rows(k, place(c, b, 0), tokens), ys_send.at[k], y_recv.at[k, b],
                   {"context": ctx(a, u, c)}).start()

    def side_moves(k):
        for u in others(b, B):
            got = rows(k, place(c, u, 0), tokens)
            remote(got, got, ys_send.at[k], y_recv.at[k, u], {"context": me}).wait_recv()
            remote(rows(k, place(c, u, 0), side), rows(k, place(c, u, 1), side), z_send.at[k], p_recv.at[k, u],
                   {"context": ctx(pair, b, c)}).start()

    def column_moves(k, d):
        for sign in (1, -1):
            t = a + sign * d

            @pl.when(inside(t))
            def _():
                s = slot(a, t)
                got = rows(k, place(c, b, s), tokens)
                remote(got, got, z_send.at[k], z_recv.at[k, s], {"context": me}).wait_recv()

                @pl.when(inside(a - sign))
                def _():
                    z_move(got, k, t, a - sign).start()

    def to_sibling(k, u):
        whole = rows(k, place(c, u, 0), line)
        remote(whole, whole, ys_send.at[k], s_recv.at[k], {"context": ctx(a, b, 1 - c)}).start()

    def rest(k, u):
        return rows(k, place(c, u, 1) + side, line - tokens - side)

    def line_moves(k):
        for u in others(b, B):
            remote(rest(k, b), rest(k, b), ys_send.at[k], f_recv.at[k, b], {"context": ctx(a, u, c)}).start()
        own_copy(k).wait()
        to_sibling(k, b)

    def plane_moves(k):
        for u in others(b, B):
            remote(rest(k, u), rest(k, u), ys_send.at[k], f_recv.at[k, u], {"context": me}).wait_recv()
            late = rows(k, place(c, u, 1), side)
            remote(late, late, z_send.at[k], p_recv.at[k, u], {"context": me}).wait_recv()
            to_sibling(k, u)

    def act_move(i, target):
        where = (c * B + b) * A + slot(target // (CORES * B), a)
        return remote(a_in.at[:, head_cols(target)], acts.at[where], a_send, a_recv, {"context": target})

    def x_moves(k):
        for r in others(rep, dp):
            remote(part.at[rep, k], part.at[rep, k], x_send.at[k], x_recv.at[k], {"dp": r}).start()

    for k in range(AHEAD):
        z_own(k)
    targets = others(me, n)
    for i, t in enumerate(targets):
        act_move(i, t).start()
    for k in range(AHEAD_Y):
        y_own(k)

    def compute(k):
        theirs = rows(k, place(1 - c, 0, 0), half)
        remote(theirs, theirs, ys_send.at[k], s_recv.at[k], {"context": me}).wait_recv()

        @pl.when(k == 0)
        def _():
            own_act.wait()
            w_copy.wait()
            most = acts.at[pl.ds(0, n - 1)]
            remote(most, most, a_send, a_recv, {"context": me}).wait_recv()
            for j in range(n):
                acts_t[:, j * tokens:(j + 1) * tokens] = acts[j].T
            acc[...] = jnp.zeros_like(acc)

        part[rep, k] = jnp.dot(acts_t[...], gath[k], preferred_element_type=jnp.float32).astype(part.dtype)
        x_moves(k)

        @pl.loop(0, CORES * B)
        def _(i):
            r = pl.ds(pl.multiple_of(i * line, line), line)
            total = acc[r] + lax.dot_general(
                gath[k, r], w[:, cols(k)], (((1,), (1,)), ((), ())), preferred_element_type=jnp.float32)

            @pl.when(k < chunks - 1)
            def _():
                acc[r] = total

            @pl.when(k == chunks - 1)
            def _():
                c_, u = i // B, lax.rem(i, B)
                for s in range(A):
                    to = ctx(slot(a, s), u, c_) * tokens
                    o_attn[pl.ds(pl.multiple_of(to, tokens), tokens)] = total[
                        s * tokens:(s + 1) * tokens].astype(o_attn.dtype)

    def finish(k):
        last = part.at[pl.ds(0, dp - 1), k]
        remote(last, last, x_send.at[k], x_recv.at[k], {"dp": rep}).wait_recv()
        total = part[0, k].astype(jnp.float32)
        for r in range(1, dp):
            total += part[r, k].astype(jnp.float32)
        o_w[:, cols(k)] = total.astype(o_w.dtype)

    def stage(k, f):
        pl.when(jnp.logical_and(k >= 0, k < chunks))(functools.partial(f, k))

    depth = HOP * (A - 2)

    @pl.loop(0, chunks + depth + PLANE + 2)
    def _(i):
        stage(i + AHEAD, z_own)
        stage(i + AHEAD_Y, y_own)
        for d in range(1, A):
            stage(i - HOP * (d - 1), lambda k, d=d: column_moves(k, d))
            if d == 1:
                stage(i, side_moves)
        stage(i - depth, line_moves)
        stage(i - depth - PLANE - 1, compute)
        stage(i - depth - PLANE, plane_moves)
        stage(i - depth - PLANE - 2, finish)

    edge = jnp.logical_or(a == 0, a == A - 1)

    def sent(ref, sem):
        remote(ref, ref, sem, s_recv.at[0], {"context": me}).wait_send()

    @pl.loop(0, chunks)
    def _(k):
        sent(rows(k, 0, half + (B - 1) * (line - side)), ys_send.at[k])
        sent(part.at[pl.ds(0, dp - 1), k], x_send.at[k])

        @pl.when(edge)
        def _():
            sent(rows(k, 0, tokens + (B - 1) * side), z_send.at[k])

        @pl.when(jnp.logical_not(edge))
        def _():
            sent(rows(k, 0, (A + 1) * tokens + (B - 1) * side), z_send.at[k])

    sent(acts.at[pl.ds(0, n - 1)], a_send)


def local(dp, n, grad_out, attn, w_out):
    g, x = grad_out[0], attn[0]
    tokens, width = g.shape
    heads = w_out.shape[0]
    length = tokens * n
    chunks = CHUNKS
    F = width // chunks
    A, B = grid_of(n // CORES)
    any_ = pl.BlockSpec(memory_space=pl.ANY)
    vmem = pl.BlockSpec(memory_space=pltpu.VMEM)
    bf = jnp.bfloat16
    dma = pltpu.SemaphoreType.DMA
    h, gw = pl.pallas_call(
        functools.partial(kernel, dp, n, chunks),
        out_shape=(jax.ShapeDtypeStruct((length, heads), bf), jax.ShapeDtypeStruct((heads, width), bf)),
        in_specs=[any_] * 3,
        out_specs=(vmem, vmem),
        scratch_shapes=[
            pltpu.VMEM((chunks, length, F), bf),
            pltpu.VMEM((n, tokens, heads), bf),
            pltpu.VMEM((heads, length), bf),
            pltpu.VMEM((heads, width), bf),
            pltpu.VMEM((length, heads), jnp.float32),
            pltpu.VMEM((dp, chunks, heads, F), bf),
            dma((chunks,)), dma((chunks, A)), dma((chunks, B)), dma((chunks,)), dma((chunks, B)), dma((chunks, B)),
            dma((chunks,)), dma, dma, dma((chunks,)), dma((chunks,)),
            dma((chunks,)), dma, dma,
        ],
        compiler_params=pltpu.CompilerParams(
            collective_id=0, has_side_effects=True, vmem_limit_bytes=52 * 2**20),
    )(g, x, w_out)
    return h[None], gw


def solution(mesh):
    dp, n = mesh.shape["dp"], mesh.shape["context"]
    in_specs = (P("dp", "context", None), P("dp", "context", None), P("context", None))
    out_specs = (P("dp", None, "context"), P("context", None))
    return jax.shard_map(functools.partial(local, dp, n), mesh=mesh, in_specs=in_specs, out_specs=out_specs,
                         check_vma=False)
```

```python
import functools

import jax
import jax.numpy as jnp
from jax import lax
from jax.experimental import pallas as pl
from jax.experimental.pallas import tpu as pltpu
from jax.sharding import PartitionSpec as P

CHUNKS = 16
AHEAD = 3
AHEAD_Y = 8
CORES = 2
SIDE = 2
ACT0 = 1
RELAY = 3
FIRST = 2
BEGIN = 7
HOP = 1
PLANE = 1
MESH = pl.DeviceIdType.MESH


def grid_of(chips):
    fast = 1
    while (2 * fast) * (2 * fast) <= chips:
        fast *= 2
    return chips // fast, fast


def side_rows(tokens):
    return tokens * SIDE // 16


def kernel(dp, n, chunks, g_in, a_in, w_in, o_attn, o_w, gath, acts, acts_t, w, acc, part,
           relay, z_send, z_recv, p_recv, ys_send, y_recv, f_recv, s_recv, a_send, a_recv, r_send, r_recv, x_send, x_recv,
           own_sem, w_sem, own_a_sem):
    A, B = grid_of(n // CORES)
    tokens, width = g_in.shape
    heads = w_in.shape[0]
    F = width // chunks
    side = side_rows(tokens)
    line = A * tokens
    half = B * line
    me = lax.axis_index("context")
    rep = lax.axis_index("dp")
    c = lax.rem(me, CORES)
    b = lax.rem(me // CORES, B)
    a = me // (CORES * B)

    def ctx(a_, b_, c_):
        return (a_ * B + b_) * CORES + c_

    def others(i, size):
        return [lax.rem(i + d, size) for d in range(1, size)]

    def slot(i, t):
        s, bit = 0, 1
        while bit < A:
            s = s + bit * lax.rem(i // bit + t // bit, 2)
            bit *= 2
        return s

    pair = a + 1 - 2 * lax.rem(a, 2)

    def cols(k):
        return pl.ds(pl.multiple_of(k * F, F), F)

    def place(c_, u, s):
        return ((c_ * B + u) * A + s) * tokens

    def rows(k, lo, size):
        return gath.at[k, pl.ds(pl.multiple_of(lo, 8), size)]

    def own(k):
        return g_in.at[:, cols(k)]

    def remote(src, dst, send, recv, target):
        return pltpu.make_async_remote_copy(
            src_ref=src, dst_ref=dst, send_sem=send, recv_sem=recv, device_id=target, device_id_type=MESH)

    def inside(t):
        return jnp.logical_and(t >= 0, t < A)

    def own_copy(k):
        return pltpu.make_async_copy(own(k), rows(k, place(c, b, 0), tokens), own_sem.at[k])

    w_copy = pltpu.make_async_copy(w_in, w, w_sem)

    def head_cols(j):
        return pl.ds(pl.multiple_of(j * heads, heads), heads)

    own_act = pltpu.make_async_copy(a_in.at[:, head_cols(me)], acts.at[(c * B + b) * A], own_a_sem)

    barrier = pltpu.get_barrier_semaphore()
    for j in others(me, n):
        pl.semaphore_signal(barrier, inc=1, device_id={"context": j}, device_id_type=MESH)
    for r in others(rep, dp):
        pl.semaphore_signal(barrier, inc=1, device_id={"dp": r}, device_id_type=MESH)
    own_act.start()
    w_copy.start()

    @pl.loop(0, chunks)
    def _(k):
        own_copy(k).start()

    pl.semaphore_wait(barrier, n - 1 + dp - 1)

    edge = jnp.logical_or(a == 0, a == A - 1)

    def by_row(f, outer, inner):
        pl.when(edge)(lambda: f(outer))
        pl.when(jnp.logical_not(edge))(lambda: f(inner))

    def z_move(src, k, t, target):
        s = slot(target, t)
        return remote(src, rows(k, place(c, b, s), tokens), z_send.at[k], z_recv.at[k, s],
                      {"context": ctx(target, b, c)})

    def z_own(k):
        for sign in (1, -1):
            @pl.when(inside(a + sign))
            def _():
                z_move(own(k), k, a, a + sign).start()

    def y_own(k):
        for u in others(b, B):
            remote(own(k), rows(k, place(c, b, 0), tokens), ys_send.at[k], y_recv.at[k, b],
                   {"context": ctx(a, u, c)}).start()

    def side_moves(k):
        for u in others(b, B):
            got = rows(k, place(c, u, 0), tokens)
            remote(got, got, ys_send.at[k], y_recv.at[k, u], {"context": me}).wait_recv()
            by_row(lambda size, u=u: remote(
                rows(k, place(c, u, 0), size), rows(k, place(c, u, 1), size), z_send.at[k], p_recv.at[k, u],
                {"context": ctx(pair, b, c)}).start(), tokens, side)

    def column_moves(k, d):
        for sign in (1, -1):
            t = a + sign * d

            @pl.when(inside(t))
            def _():
                s = slot(a, t)
                got = rows(k, place(c, b, s), tokens)
                remote(got, got, z_send.at[k], z_recv.at[k, s], {"context": me}).wait_recv()

                @pl.when(inside(a - sign))
                def _():
                    z_move(got, k, t, a - sign).start()

    def to_sibling(k, u):
        whole = rows(k, place(c, u, 0), line)
        remote(whole, whole, ys_send.at[k], s_recv.at[k], {"context": ctx(a, b, 1 - c)}).start()

    def across(k, s):
        def send(skip):
            if skip < tokens:
                ref = rows(k, place(c, b, s) + skip, tokens - skip)
                for u in others(b, B):
                    remote(ref, ref, ys_send.at[k], f_recv.at[k, b], {"context": ctx(a, u, c)}).start()
        if s == 1:
            by_row(send, side, tokens)
        else:
            send(0)

    def line_moves(k):
        own_copy(k).wait()
        to_sibling(k, b)

    def plane_moves(k):
        for u in others(b, B):
            def wait(size, u=u):
                late = rows(k, place(c, u, 1), size)
                remote(late, late, z_send.at[k], p_recv.at[k, u], {"context": me}).wait_recv()
                rest = rows(k, place(c, u, 1) + size, line - tokens - size)
                remote(rest, rest, ys_send.at[k], f_recv.at[k, u], {"context": me}).wait_recv()
            by_row(wait, side, tokens)
            to_sibling(k, u)

    def act_move(target):
        where = (c * B + b) * A + slot(target // (CORES * B), a)
        return remote(a_in.at[:, head_cols(target)], acts.at[where], a_send, a_recv, {"context": target})

    def x_moves(k):
        for r in others(rep, dp):
            remote(part.at[rep, k], part.at[rep, k], x_send.at[k], x_recv.at[k], {"dp": r}).start()

    for k in range(AHEAD):
        z_own(k)
    def edges():
        return [(e, c_) for e in range(2) for c_ in range(CORES)]

    def relay_out():
        for u in others(b, B):
            for e, c_ in edges():
                remote(a_in.at[:, head_cols(ctx(e * (A - 1), u, c_))], relay.at[b, e, c_], a_send, r_recv.at[b],
                       {"context": ctx(a, u, c)}).start()

    def relay_on():
        for u in others(b, B):
            remote(relay.at[u], relay.at[u], a_send, r_recv.at[u], {"context": me}).wait_recv()
            for e, c_ in edges():
                remote(relay.at[u, e, c_], acts.at[(c * B + u) * A + slot(e * (A - 1), a)], r_send, a_recv,
                       {"context": ctx(e * (A - 1), b, c_)}).start()

    def inner(f, also=True):
        if A > 2:
            pl.when(jnp.logical_and(jnp.logical_not(edge), also))(f)

    act_move(ctx(a, b, 1 - c)).start()
    for k in range(AHEAD_Y):
        if k == FIRST:
            inner(relay_out)
        y_own(k)

    depth = HOP * (A - 2)
    lag = depth + PLANE + 1
    chips = n // CORES
    batch = -(-(chips - 1) // (lag - ACT0))

    def act_moves(i):
        for q in range(batch):
            d = (i - ACT0) * batch + q + 1
            to = lax.rem(me // CORES + d, chips)
            direct = jnp.logical_and(i >= ACT0, d < chips)
            if A > 2:
                t = to // B
                last = jnp.logical_or(t == 0, t == A - 1)
                direct = jnp.logical_and(direct, jnp.logical_or(
                    edge, jnp.logical_or(jnp.logical_not(last), lax.rem(to, B) == b)))

            @pl.when(direct)
            def _():
                for c_ in range(CORES):
                    act_move(to * CORES + c_).start()
        inner(relay_on, i == RELAY)

    def ready(k):
        theirs = rows(k, place(1 - c, 0, 0), half)
        remote(theirs, theirs, ys_send.at[k], s_recv.at[k], {"context": me}).wait_recv()

    def weights(k):
        @pl.when(k == 0)
        def _():
            own_act.wait()
            most = acts.at[pl.ds(0, n - 1)]
            remote(most, most, a_send, a_recv, {"context": me}).wait_recv()
            for j in range(n):
                acts_t[:, j * tokens:(j + 1) * tokens] = acts[j].T

        part[rep, k] = jnp.dot(acts_t[...], gath[k], preferred_element_type=jnp.float32).astype(part.dtype)
        x_moves(k)

    def inputs(k):
        @pl.when(k == 0)
        def _():
            w_copy.wait()
            acc[...] = jnp.zeros_like(acc)

        @pl.loop(0, CORES * B)
        def _(i):
            r = pl.ds(pl.multiple_of(i * line, line), line)
            total = acc[r] + lax.dot_general(
                gath[k, r], w[:, cols(k)], (((1,), (1,)), ((), ())), preferred_element_type=jnp.float32)

            @pl.when(k < chunks - 1)
            def _():
                acc[r] = total

            @pl.when(k == chunks - 1)
            def _():
                c_, u = i // B, lax.rem(i, B)
                for s in range(A):
                    to = ctx(slot(a, s), u, c_) * tokens
                    o_attn[pl.ds(pl.multiple_of(to, tokens), tokens)] = total[
                        s * tokens:(s + 1) * tokens].astype(o_attn.dtype)

    def finish(k):
        last = part.at[pl.ds(0, dp - 1), k]
        remote(last, last, x_send.at[k], x_recv.at[k], {"dp": rep}).wait_recv()
        total = part[0, k].astype(jnp.float32)
        for r in range(1, dp):
            total += part[r, k].astype(jnp.float32)
        o_w[:, cols(k)] = total.astype(o_w.dtype)

    def sent(ref, sem):
        remote(ref, ref, sem, s_recv.at[0], {"context": me}).wait_send()

    def drain(k):
        by_row(lambda size: sent(rows(k, 0, half + (B - 1) * (line - size)), ys_send.at[k]), side, tokens)
        sent(part.at[pl.ds(0, dp - 1), k], x_send.at[k])

        by_row(lambda size: sent(rows(k, 0, size), z_send.at[k]), B * tokens, (A + 1) * tokens + (B - 1) * side)

    def stage(k, f):
        pl.when(jnp.logical_and(k >= 0, k < chunks))(functools.partial(f, k))

    def summed(i):
        return jnp.clip(jnp.minimum(i - lag + 1, 2 * (i - BEGIN + 1)), 0, chunks)

    @pl.loop(0, chunks + lag + 1)
    def _(i):
        for d in range(A - 1, 0, -1):
            stage(i - HOP * (d - 1), lambda k, d=d: column_moves(k, d))
            stage(i - HOP * (d - 1), lambda k, d=d: across(k, d))
        stage(i, side_moves)
        stage(i + AHEAD, z_own)
        stage(i + AHEAD_Y, y_own)
        act_moves(i)
        stage(i - depth, line_moves)
        stage(i - lag, ready)

        @pl.loop(summed(i - 1), summed(i))
        def _(k):
            weights(k)

        stage(i - lag, inputs)
        stage(i - depth - PLANE, plane_moves)

        @pl.loop(summed(i - 2), summed(i - 1))
        def _(k):
            finish(k)
            drain(k)

    sent(acts.at[pl.ds(0, n - 1)], a_send)
    inner(lambda: sent(relay.at[pl.ds(0, B - 1)], r_send))


def store(h, gw, o_h, o_gw, sem):
    moves = [pltpu.make_async_copy(h, o_h, sem.at[0]), pltpu.make_async_copy(gw, o_gw, sem.at[1])]
    for m in moves:
        m.start()
    for m in moves:
        m.wait()


def local(dp, n, grad_out, attn, w_out):
    g, x = grad_out[0], attn[0]
    tokens, width = g.shape
    heads = w_out.shape[0]
    length = tokens * n
    chunks = CHUNKS
    F = width // chunks
    A, B = grid_of(n // CORES)
    scratch = 2 * (length * width + 2 * length * heads + heads * width * (1 + dp)) + 4 * length * heads
    limit = min(52 * 2**20, scratch + 10 * 2**20)
    any_ = pl.BlockSpec(memory_space=pl.ANY)
    vmem = pl.BlockSpec(memory_space=pltpu.VMEM)
    bf = jnp.bfloat16
    dma = pltpu.SemaphoreType.DMA
    h, gw = pl.pallas_call(
        functools.partial(kernel, dp, n, chunks),
        out_shape=(jax.ShapeDtypeStruct((length, heads), bf), jax.ShapeDtypeStruct((heads, width), bf)),
        in_specs=[any_] * 3,
        out_specs=(vmem, vmem),
        scratch_shapes=[
            pltpu.VMEM((chunks, length, F), bf),
            pltpu.VMEM((n, tokens, heads), bf),
            pltpu.VMEM((heads, length), bf),
            pltpu.VMEM((heads, width), bf),
            pltpu.VMEM((length, heads), jnp.float32),
            pltpu.VMEM((dp, chunks, heads, F), bf),
            pltpu.VMEM((B, 2, CORES, tokens, heads), bf),
            dma((chunks,)), dma((chunks, A)), dma((chunks, B)), dma((chunks,)), dma((chunks, B)), dma((chunks, B)),
            dma((chunks,)), dma, dma, dma, dma((B,)), dma((chunks,)), dma((chunks,)),
            dma((chunks,)), dma, dma,
        ],
        compiler_params=pltpu.CompilerParams(
            collective_id=0, has_side_effects=True, vmem_limit_bytes=limit),
    )(*[pltpu.with_memory_space_constraint(v, pltpu.HBM) for v in (g, x, w_out)])
    h, gw = pl.pallas_call(
        store,
        out_shape=(jax.ShapeDtypeStruct((length, heads), bf), jax.ShapeDtypeStruct((heads, width), bf)),
        in_specs=[any_] * 2,
        out_specs=(any_, any_),
        scratch_shapes=[dma((2,))],
        compiler_params=pltpu.CompilerParams(vmem_limit_bytes=8 * 2**20),
    )(h, gw)
    return h[None], gw


def solution(mesh):
    dp, n = mesh.shape["dp"], mesh.shape["context"]
    in_specs = (P("dp", "context", None), P("dp", "context", None), P("context", None))
    out_specs = (P("dp", None, "context"), P("context", None))
    return jax.shard_map(functools.partial(local, dp, n), mesh=mesh, in_specs=in_specs, out_specs=out_specs,
                         check_vma=False)
```

```python
import functools

import jax
import jax.numpy as jnp
from jax import lax
from jax.experimental import pallas as pl
from jax.experimental.pallas import tpu as pltpu
from jax.sharding import PartitionSpec as P

CHUNKS = 16
AHEAD = 3
AHEAD_Y = 8
CORES = 2
SIDE = 2
ACT0 = 1
RELAY = 3
FIRST = 4
BEGIN = 7
HOP = 1
PLANE = 1
MESH = pl.DeviceIdType.MESH


def grid_of(chips):
    fast = 1
    while (2 * fast) * (2 * fast) <= chips:
        fast *= 2
    return chips // fast, fast


def side_rows(tokens):
    return tokens * SIDE // 16


def kernel(dp, n, chunks, g_in, a_in, w_in, o_attn, o_w, gath, acts, acts_t, w, acc, part,
           relay, z_send, z_recv, p_recv, ys_send, y_recv, f_recv, s_recv, a_send, a_recv, r_send, r_recv, x_send, x_recv,
           own_sem, w_sem, own_a_sem):
    A, B = grid_of(n // CORES)
    tokens, width = g_in.shape
    heads = w_in.shape[0]
    F = width // chunks
    side = side_rows(tokens)
    line = A * tokens
    half = B * line
    me = lax.axis_index("context")
    rep = lax.axis_index("dp")
    c = lax.rem(me, CORES)
    b = lax.rem(me // CORES, B)
    a = me // (CORES * B)

    def ctx(a_, b_, c_):
        return (a_ * B + b_) * CORES + c_

    def others(i, size):
        return [lax.rem(i + d, size) for d in range(1, size)]

    def slot(i, t):
        s, bit = 0, 1
        while bit < A:
            s = s + bit * lax.rem(i // bit + t // bit, 2)
            bit *= 2
        return s

    pair = a + 1 - 2 * lax.rem(a, 2)

    def cols(k):
        return pl.ds(pl.multiple_of(k * F, F), F)

    def place(c_, u, s):
        return ((c_ * B + u) * A + s) * tokens

    def rows(k, lo, size):
        return gath.at[k, pl.ds(pl.multiple_of(lo, 8), size)]

    def own(k):
        return g_in.at[:, cols(k)]

    def remote(src, dst, send, recv, target):
        return pltpu.make_async_remote_copy(
            src_ref=src, dst_ref=dst, send_sem=send, recv_sem=recv, device_id=target, device_id_type=MESH)

    def inside(t):
        return jnp.logical_and(t >= 0, t < A)

    def own_copy(k):
        return pltpu.make_async_copy(own(k), rows(k, place(c, b, 0), tokens), own_sem.at[k])

    w_copy = pltpu.make_async_copy(w_in, w, w_sem)

    def head_cols(j):
        return pl.ds(pl.multiple_of(j * heads, heads), heads)

    own_act = pltpu.make_async_copy(a_in.at[:, head_cols(me)], acts.at[(c * B + b) * A], own_a_sem)

    barrier = pltpu.get_barrier_semaphore()
    for j in others(me, n):
        pl.semaphore_signal(barrier, inc=1, device_id={"context": j}, device_id_type=MESH)
    for r in others(rep, dp):
        pl.semaphore_signal(barrier, inc=1, device_id={"dp": r}, device_id_type=MESH)
    own_act.start()
    w_copy.start()

    @pl.loop(0, chunks)
    def _(k):
        own_copy(k).start()

    pl.semaphore_wait(barrier, n - 1 + dp - 1)

    edge = jnp.logical_or(a == 0, a == A - 1)

    def by_row(f, outer, inner):
        pl.when(edge)(lambda: f(outer))
        pl.when(jnp.logical_not(edge))(lambda: f(inner))

    def z_move(src, k, t, target):
        s = slot(target, t)
        return remote(src, rows(k, place(c, b, s), tokens), z_send.at[k], z_recv.at[k, s],
                      {"context": ctx(target, b, c)})

    def z_own(k):
        for sign in (1, -1):
            @pl.when(inside(a + sign))
            def _():
                z_move(own(k), k, a, a + sign).start()

    def y_own(k):
        for u in others(b, B):
            remote(own(k), rows(k, place(c, b, 0), tokens), ys_send.at[k], y_recv.at[k, b],
                   {"context": ctx(a, u, c)}).start()

    def side_moves(k):
        for u in others(b, B):
            got = rows(k, place(c, u, 0), tokens)
            remote(got, got, ys_send.at[k], y_recv.at[k, u], {"context": me}).wait_recv()
            by_row(lambda size, u=u: remote(
                rows(k, place(c, u, 0), size), rows(k, place(c, u, 1), size), z_send.at[k], p_recv.at[k, u],
                {"context": ctx(pair, b, c)}).start(), tokens, side)

    def column_moves(k, d):
        for sign in (1, -1):
            t = a + sign * d

            @pl.when(inside(t))
            def _():
                s = slot(a, t)
                got = rows(k, place(c, b, s), tokens)
                remote(got, got, z_send.at[k], z_recv.at[k, s], {"context": me}).wait_recv()

                @pl.when(inside(a - sign))
                def _():
                    z_move(got, k, t, a - sign).start()

    def to_sibling(k, u):
        whole = rows(k, place(c, u, 0), line)
        remote(whole, whole, ys_send.at[k], s_recv.at[k], {"context": ctx(a, b, 1 - c)}).start()

    def across(k, s):
        def send(skip):
            if skip < tokens:
                ref = rows(k, place(c, b, s) + skip, tokens - skip)
                for u in others(b, B):
                    remote(ref, ref, ys_send.at[k], f_recv.at[k, b], {"context": ctx(a, u, c)}).start()
        if s == 1:
            by_row(send, side, tokens)
        else:
            send(0)

    def line_moves(k):
        own_copy(k).wait()
        to_sibling(k, b)

    def plane_moves(k):
        for u in others(b, B):
            def wait(size, u=u):
                late = rows(k, place(c, u, 1), size)
                remote(late, late, z_send.at[k], p_recv.at[k, u], {"context": me}).wait_recv()
                rest = rows(k, place(c, u, 1) + size, line - tokens - size)
                remote(rest, rest, ys_send.at[k], f_recv.at[k, u], {"context": me}).wait_recv()
            by_row(wait, side, tokens)
            to_sibling(k, u)

    def act_move(target):
        where = (c * B + b) * A + slot(target // (CORES * B), a)
        return remote(a_in.at[:, head_cols(target)], acts.at[where], a_send, a_recv, {"context": target})

    def x_moves(k):
        for r in others(rep, dp):
            remote(part.at[rep, k], part.at[rep, k], x_send.at[k], x_recv.at[k], {"dp": r}).start()

    for k in range(AHEAD):
        z_own(k)
    def edges():
        return [(e, c_) for e in range(2) for c_ in range(CORES)]

    def relay_out():
        for u in others(b, B):
            for e, c_ in edges():
                remote(a_in.at[:, head_cols(ctx(e * (A - 1), u, c_))], relay.at[b, e, c_], a_send, r_recv.at[b],
                       {"context": ctx(a, u, c)}).start()

    def relay_on():
        for u in others(b, B):
            remote(relay.at[u], relay.at[u], a_send, r_recv.at[u], {"context": me}).wait_recv()
            for e, c_ in edges():
                remote(relay.at[u, e, c_], acts.at[(c * B + u) * A + slot(e * (A - 1), a)], r_send, a_recv,
                       {"context": ctx(e * (A - 1), b, c_)}).start()

    def inner(f, also=True):
        if A > 2:
            pl.when(jnp.logical_and(jnp.logical_not(edge), also))(f)

    act_move(ctx(a, b, 1 - c)).start()
    for k in range(AHEAD_Y):
        if k == FIRST:
            inner(relay_out)
        y_own(k)

    depth = HOP * (A - 2)
    lag = depth + PLANE + 1
    chips = n // CORES
    batch = -(-(chips - 1) // (lag - ACT0))

    def act_moves(i):
        for q in range(batch):
            d = (i - ACT0) * batch + q + 1
            to = lax.rem(me // CORES + d, chips)
            direct = jnp.logical_and(i >= ACT0, d < chips)
            if A > 2:
                t = to // B
                last = jnp.logical_or(t == 0, t == A - 1)
                direct = jnp.logical_and(direct, jnp.logical_or(
                    edge, jnp.logical_or(jnp.logical_not(last), lax.rem(to, B) == b)))

            @pl.when(direct)
            def _():
                for c_ in range(CORES):
                    act_move(to * CORES + c_).start()
        inner(relay_on, i == RELAY)

    def ready(k):
        theirs = rows(k, place(1 - c, 0, 0), half)
        remote(theirs, theirs, ys_send.at[k], s_recv.at[k], {"context": me}).wait_recv()

    def weights(k):
        @pl.when(k == 0)
        def _():
            own_act.wait()
            most = acts.at[pl.ds(0, n - 1)]
            remote(most, most, a_send, a_recv, {"context": me}).wait_recv()
            for j in range(n):
                acts_t[:, j * tokens:(j + 1) * tokens] = acts[j].T

        part[rep, k] = jnp.dot(acts_t[...], gath[k], preferred_element_type=jnp.float32).astype(part.dtype)
        x_moves(k)

    def inputs(k):
        @pl.when(k == 0)
        def _():
            w_copy.wait()
            acc[...] = jnp.zeros_like(acc)

        @pl.loop(0, CORES * B)
        def _(i):
            r = pl.ds(pl.multiple_of(i * line, line), line)
            total = acc[r] + lax.dot_general(
                gath[k, r], w[:, cols(k)], (((1,), (1,)), ((), ())), preferred_element_type=jnp.float32)

            @pl.when(k < chunks - 1)
            def _():
                acc[r] = total

            @pl.when(k == chunks - 1)
            def _():
                c_, u = i // B, lax.rem(i, B)
                for s in range(A):
                    to = ctx(slot(a, s), u, c_) * tokens
                    o_attn[pl.ds(pl.multiple_of(to, tokens), tokens)] = total[
                        s * tokens:(s + 1) * tokens].astype(o_attn.dtype)

    def finish(k):
        last = part.at[pl.ds(0, dp - 1), k]
        remote(last, last, x_send.at[k], x_recv.at[k], {"dp": rep}).wait_recv()
        total = part[0, k].astype(jnp.float32)
        for r in range(1, dp):
            total += part[r, k].astype(jnp.float32)
        o_w[:, cols(k)] = total.astype(o_w.dtype)

    def sent(ref, sem):
        remote(ref, ref, sem, s_recv.at[0], {"context": me}).wait_send()

    def drain(k):
        by_row(lambda size: sent(rows(k, 0, half + (B - 1) * (line - size)), ys_send.at[k]), side, tokens)
        sent(part.at[pl.ds(0, dp - 1), k], x_send.at[k])

        by_row(lambda size: sent(rows(k, 0, size), z_send.at[k]), B * tokens, (A + 1) * tokens + (B - 1) * side)

    def stage(k, f):
        pl.when(jnp.logical_and(k >= 0, k < chunks))(functools.partial(f, k))

    def summed(i):
        return jnp.clip(jnp.minimum(i - lag + 1, 2 * (i - BEGIN + 1)), 0, chunks)

    @pl.loop(0, chunks + lag + 2)
    def _(i):
        for d in range(A - 1, 0, -1):
            stage(i - HOP * (d - 1), lambda k, d=d: column_moves(k, d))
            stage(i - HOP * (d - 1), lambda k, d=d: across(k, d))
        stage(i, side_moves)
        act_moves(i)
        stage(i + AHEAD, z_own)
        stage(i + AHEAD_Y, y_own)
        stage(i - depth, line_moves)
        stage(i - lag, ready)

        @pl.loop(summed(i - 1), summed(i))
        def _(k):
            weights(k)

        stage(i - lag, inputs)
        stage(i - depth - PLANE, plane_moves)

        @pl.loop(summed(i - 3), summed(i - 2))
        def _(k):
            finish(k)
            drain(k)

    sent(acts.at[pl.ds(0, n - 1)], a_send)
    inner(lambda: sent(relay.at[pl.ds(0, B - 1)], r_send))


def store(h, gw, o_h, o_gw, sem):
    moves, half = [], sem.shape[0] // 2
    for src, dst in ((gw, o_gw), (h, o_h)):
        size = src.shape[0] // half
        for i in range(half):
            r = pl.ds(i * size, size)
            moves.append(pltpu.make_async_copy(src.at[r], dst.at[r], sem.at[len(moves)]))
    for m in moves:
        m.start()
    for m in moves:
        m.wait()


def local(dp, n, grad_out, attn, w_out):
    g, x = grad_out[0], attn[0]
    tokens, width = g.shape
    heads = w_out.shape[0]
    length = tokens * n
    chunks = CHUNKS
    F = width // chunks
    A, B = grid_of(n // CORES)
    scratch = 2 * (length * width + 2 * length * heads + heads * width * (1 + dp)) + 4 * length * heads
    limit = min(52 * 2**20, scratch + 10 * 2**20)
    any_ = pl.BlockSpec(memory_space=pl.ANY)
    vmem = pl.BlockSpec(memory_space=pltpu.VMEM)
    bf = jnp.bfloat16
    dma = pltpu.SemaphoreType.DMA
    h, gw = pl.pallas_call(
        functools.partial(kernel, dp, n, chunks),
        out_shape=(jax.ShapeDtypeStruct((length, heads), bf), jax.ShapeDtypeStruct((heads, width), bf)),
        in_specs=[any_] * 3,
        out_specs=(vmem, vmem),
        scratch_shapes=[
            pltpu.VMEM((chunks, length, F), bf),
            pltpu.VMEM((n, tokens, heads), bf),
            pltpu.VMEM((heads, length), bf),
            pltpu.VMEM((heads, width), bf),
            pltpu.VMEM((length, heads), jnp.float32),
            pltpu.VMEM((dp, chunks, heads, F), bf),
            pltpu.VMEM((B, 2, CORES, tokens, heads), bf),
            dma((chunks,)), dma((chunks, A)), dma((chunks, B)), dma((chunks,)), dma((chunks, B)), dma((chunks, B)),
            dma((chunks,)), dma, dma, dma, dma((B,)), dma((chunks,)), dma((chunks,)),
            dma((chunks,)), dma, dma,
        ],
        compiler_params=pltpu.CompilerParams(
            collective_id=0, has_side_effects=True, vmem_limit_bytes=limit),
    )(*[pltpu.with_memory_space_constraint(v, pltpu.HBM) for v in (g, x, w_out)])
    h, gw = pl.pallas_call(
        store,
        out_shape=(jax.ShapeDtypeStruct((length, heads), bf), jax.ShapeDtypeStruct((heads, width), bf)),
        in_specs=[any_] * 2,
        out_specs=(any_, any_),
        scratch_shapes=[dma((8,))],
        compiler_params=pltpu.CompilerParams(vmem_limit_bytes=8 * 2**20),
    )(h, gw)
    return h[None], gw


def solution(mesh):
    dp, n = mesh.shape["dp"], mesh.shape["context"]
    in_specs = (P("dp", "context", None), P("dp", "context", None), P("context", None))
    out_specs = (P("dp", None, "context"), P("context", None))
    return jax.shard_map(functools.partial(local, dp, n), mesh=mesh, in_specs=in_specs, out_specs=out_specs,
                         check_vma=False)
```

```python
import functools

import jax
import jax.numpy as jnp
from jax import lax
from jax.experimental import pallas as pl
from jax.experimental.pallas import tpu as pltpu
from jax.sharding import PartitionSpec as P

CHUNKS = 16
AHEAD = 3
AHEAD_Y = 8
CORES = 2
SIDE = 2
ACT0 = 1
RELAY = 2
FIRST = 4
BEGIN = 7
HOP = 1
PLANE = 1
MESH = pl.DeviceIdType.MESH


def grid_of(chips):
    fast = 1
    while (2 * fast) * (2 * fast) <= chips:
        fast *= 2
    return chips // fast, fast


def side_rows(tokens):
    return tokens * SIDE // 16


def kernel(dp, n, chunks, g_in, a_in, w_in, o_attn, o_w, gath, acts, acts_t, w, acc, part,
           relay, z_send, z_recv, p_recv, ys_send, y_recv, f_recv, s_recv, a_send, a_recv, r_send, r_recv, x_send, x_recv,
           own_sem, w_sem, own_a_sem):
    A, B = grid_of(n // CORES)
    tokens, width = g_in.shape
    heads = w_in.shape[0]
    F = width // chunks
    side = side_rows(tokens)
    line = A * tokens
    half = B * line
    me = lax.axis_index("context")
    rep = lax.axis_index("dp")
    c = lax.rem(me, CORES)
    b = lax.rem(me // CORES, B)
    a = me // (CORES * B)

    def ctx(a_, b_, c_):
        return (a_ * B + b_) * CORES + c_

    def others(i, size):
        return [lax.rem(i + d, size) for d in range(1, size)]

    def slot(i, t):
        s, bit = 0, 1
        while bit < A:
            s = s + bit * lax.rem(i // bit + t // bit, 2)
            bit *= 2
        return s

    pair = a + 1 - 2 * lax.rem(a, 2)

    def cols(k):
        return pl.ds(pl.multiple_of(k * F, F), F)

    def place(c_, u, s):
        return ((c_ * B + u) * A + s) * tokens

    def rows(k, lo, size):
        return gath.at[k, pl.ds(pl.multiple_of(lo, 8), size)]

    def own(k):
        return g_in.at[:, cols(k)]

    def remote(src, dst, send, recv, target):
        return pltpu.make_async_remote_copy(
            src_ref=src, dst_ref=dst, send_sem=send, recv_sem=recv, device_id=target, device_id_type=MESH)

    def inside(t):
        return jnp.logical_and(t >= 0, t < A)

    def own_copy(k):
        return pltpu.make_async_copy(own(k), rows(k, place(c, b, 0), tokens), own_sem.at[k])

    w_copy = pltpu.make_async_copy(w_in, w, w_sem)

    def head_cols(j):
        return pl.ds(pl.multiple_of(j * heads, heads), heads)

    own_act = pltpu.make_async_copy(a_in.at[:, head_cols(me)], acts.at[(c * B + b) * A], own_a_sem)

    barrier = pltpu.get_barrier_semaphore()
    for j in others(me, n):
        pl.semaphore_signal(barrier, inc=1, device_id={"context": j}, device_id_type=MESH)
    for r in others(rep, dp):
        pl.semaphore_signal(barrier, inc=1, device_id={"dp": r}, device_id_type=MESH)
    own_act.start()
    w_copy.start()

    @pl.loop(0, chunks)
    def _(k):
        own_copy(k).start()

    pl.semaphore_wait(barrier, n - 1 + dp - 1)

    edge = jnp.logical_or(a == 0, a == A - 1)

    def by_row(f, outer, inner):
        pl.when(edge)(lambda: f(outer))
        pl.when(jnp.logical_not(edge))(lambda: f(inner))

    def z_move(src, k, t, target):
        s = slot(target, t)
        return remote(src, rows(k, place(c, b, s), tokens), z_send.at[k], z_recv.at[k, s],
                      {"context": ctx(target, b, c)})

    def z_own(k):
        for sign in (1, -1):
            @pl.when(inside(a + sign))
            def _():
                z_move(own(k), k, a, a + sign).start()

    def y_own(k):
        for u in others(b, B):
            remote(own(k), rows(k, place(c, b, 0), tokens), ys_send.at[k], y_recv.at[k, b],
                   {"context": ctx(a, u, c)}).start()

    def side_moves(k):
        for u in others(b, B):
            got = rows(k, place(c, u, 0), tokens)
            remote(got, got, ys_send.at[k], y_recv.at[k, u], {"context": me}).wait_recv()
            by_row(lambda size, u=u: remote(
                rows(k, place(c, u, 0), size), rows(k, place(c, u, 1), size), z_send.at[k], p_recv.at[k, u],
                {"context": ctx(pair, b, c)}).start(), tokens, side)

    def column_moves(k, d):
        for sign in (1, -1):
            t = a + sign * d

            @pl.when(inside(t))
            def _():
                s = slot(a, t)
                got = rows(k, place(c, b, s), tokens)
                remote(got, got, z_send.at[k], z_recv.at[k, s], {"context": me}).wait_recv()

                @pl.when(inside(a - sign))
                def _():
                    z_move(got, k, t, a - sign).start()

    def to_sibling(k, u):
        whole = rows(k, place(c, u, 0), line)
        remote(whole, whole, ys_send.at[k], s_recv.at[k], {"context": ctx(a, b, 1 - c)}).start()

    def across(k, s):
        def send(skip):
            if skip < tokens:
                ref = rows(k, place(c, b, s) + skip, tokens - skip)
                for u in others(b, B):
                    remote(ref, ref, ys_send.at[k], f_recv.at[k, b], {"context": ctx(a, u, c)}).start()
        if s == 1:
            by_row(send, side, tokens)
        else:
            send(0)

    def line_moves(k):
        own_copy(k).wait()
        to_sibling(k, b)

    def plane_moves(k):
        for u in others(b, B):
            def wait(size, u=u):
                late = rows(k, place(c, u, 1), size)
                remote(late, late, z_send.at[k], p_recv.at[k, u], {"context": me}).wait_recv()
                rest = rows(k, place(c, u, 1) + size, line - tokens - size)
                remote(rest, rest, ys_send.at[k], f_recv.at[k, u], {"context": me}).wait_recv()
            by_row(wait, side, tokens)
            to_sibling(k, u)

    def act_move(target):
        where = (c * B + b) * A + slot(target // (CORES * B), a)
        return remote(a_in.at[:, head_cols(target)], acts.at[where], a_send, a_recv, {"context": target})

    def x_moves(k):
        for r in others(rep, dp):
            remote(part.at[rep, k], part.at[rep, k], x_send.at[k], x_recv.at[k], {"dp": r}).start()

    for k in range(AHEAD):
        z_own(k)
    def edges():
        return [(e, c_) for e in range(2) for c_ in range(CORES)]

    def relay_out():
        for u in others(b, B):
            for e, c_ in edges():
                remote(a_in.at[:, head_cols(ctx(e * (A - 1), u, c_))], relay.at[b, e, c_], a_send, r_recv.at[b],
                       {"context": ctx(a, u, c)}).start()

    def relay_on():
        for u in others(b, B):
            remote(relay.at[u], relay.at[u], a_send, r_recv.at[u], {"context": me}).wait_recv()
            for e, c_ in edges():
                remote(relay.at[u, e, c_], acts.at[(c * B + u) * A + slot(e * (A - 1), a)], r_send, a_recv,
                       {"context": ctx(e * (A - 1), b, c_)}).start()

    def inner(f, also=True):
        if A > 2:
            pl.when(jnp.logical_and(jnp.logical_not(edge), also))(f)

    act_move(ctx(a, b, 1 - c)).start()
    for k in range(AHEAD_Y):
        if k == FIRST:
            inner(relay_out)
        y_own(k)

    depth = HOP * (A - 2)
    lag = depth + PLANE + 1
    chips = n // CORES
    batch = -(-(chips - 1) // (lag - ACT0))

    def act_moves(i):
        for q in range(batch):
            d = (i - ACT0) * batch + q + 1
            to = lax.rem(me // CORES + d, chips)
            direct = jnp.logical_and(i >= ACT0, d < chips)
            if A > 2:
                t = to // B
                last = jnp.logical_or(t == 0, t == A - 1)
                direct = jnp.logical_and(direct, jnp.logical_or(
                    edge, jnp.logical_or(jnp.logical_not(last), lax.rem(to, B) == b)))

            @pl.when(direct)
            def _():
                for c_ in range(CORES):
                    act_move(to * CORES + c_).start()
        inner(relay_on, i == RELAY)

    def ready(k):
        theirs = rows(k, place(1 - c, 0, 0), half)
        remote(theirs, theirs, ys_send.at[k], s_recv.at[k], {"context": me}).wait_recv()

    def weights(k):
        @pl.when(k == 0)
        def _():
            own_act.wait()
            most = acts.at[pl.ds(0, n - 1)]
            remote(most, most, a_send, a_recv, {"context": me}).wait_recv()
            for j in range(n):
                acts_t[:, j * tokens:(j + 1) * tokens] = acts[j].T

        part[rep, k] = jnp.dot(acts_t[...], gath[k], preferred_element_type=jnp.float32).astype(part.dtype)
        x_moves(k)

    def inputs(k):
        @pl.when(k == 0)
        def _():
            w_copy.wait()
            acc[...] = jnp.zeros_like(acc)

        @pl.loop(0, CORES * B)
        def _(i):
            r = pl.ds(pl.multiple_of(i * line, line), line)
            total = acc[r] + lax.dot_general(
                gath[k, r], w[:, cols(k)], (((1,), (1,)), ((), ())), preferred_element_type=jnp.float32)

            @pl.when(k < chunks - 1)
            def _():
                acc[r] = total

            @pl.when(k == chunks - 1)
            def _():
                c_, u = i // B, lax.rem(i, B)
                for s in range(A):
                    to = ctx(slot(a, s), u, c_) * tokens
                    o_attn[pl.ds(pl.multiple_of(to, tokens), tokens)] = total[
                        s * tokens:(s + 1) * tokens].astype(o_attn.dtype)

    def finish(k):
        last = part.at[pl.ds(0, dp - 1), k]
        remote(last, last, x_send.at[k], x_recv.at[k], {"dp": rep}).wait_recv()
        total = part[0, k].astype(jnp.float32)
        for r in range(1, dp):
            total += part[r, k].astype(jnp.float32)
        o_w[:, cols(k)] = total.astype(o_w.dtype)

    def sent(ref, sem):
        remote(ref, ref, sem, s_recv.at[0], {"context": me}).wait_send()

    def drain(k):
        by_row(lambda size: sent(rows(k, 0, half + (B - 1) * (line - size)), ys_send.at[k]), side, tokens)
        sent(part.at[pl.ds(0, dp - 1), k], x_send.at[k])

        by_row(lambda size: sent(rows(k, 0, size), z_send.at[k]), B * tokens, (A + 1) * tokens + (B - 1) * side)

    def stage(k, f):
        pl.when(jnp.logical_and(k >= 0, k < chunks))(functools.partial(f, k))

    def summed(i):
        return jnp.clip(jnp.minimum(i - lag + 1, 2 * (i - BEGIN + 1)), 0, chunks)

    @pl.loop(0, chunks + lag + 1)
    def _(i):
        for d in range(A - 1, 0, -1):
            stage(i - HOP * (d - 1), lambda k, d=d: column_moves(k, d))
            stage(i - HOP * (d - 1), lambda k, d=d: across(k, d))
        stage(i, side_moves)
        stage(i + AHEAD, z_own)
        stage(i + AHEAD_Y, y_own)
        act_moves(i)
        stage(i - depth, line_moves)
        stage(i - lag, ready)

        @pl.loop(summed(i - 1), summed(i))
        def _(k):
            weights(k)

        stage(i - lag, inputs)
        stage(i - depth - PLANE, plane_moves)

        @pl.loop(summed(i - 2), summed(i - 1))
        def _(k):
            finish(k)
            drain(k)

    sent(acts.at[pl.ds(0, n - 1)], a_send)
    inner(lambda: sent(relay.at[pl.ds(0, B - 1)], r_send))


def store(h, gw, o_h, o_gw, sem):
    moves = [pltpu.make_async_copy(h, o_h, sem.at[0]), pltpu.make_async_copy(gw, o_gw, sem.at[1])]
    for m in moves:
        m.start()
    for m in moves:
        m.wait()


def local(dp, n, grad_out, attn, w_out):
    g, x = grad_out[0], attn[0]
    tokens, width = g.shape
    heads = w_out.shape[0]
    length = tokens * n
    chunks = CHUNKS
    F = width // chunks
    A, B = grid_of(n // CORES)
    scratch = 2 * (length * width + 2 * length * heads + heads * width * (1 + dp)) + 4 * length * heads
    limit = min(52 * 2**20, scratch + 10 * 2**20)
    any_ = pl.BlockSpec(memory_space=pl.ANY)
    vmem = pl.BlockSpec(memory_space=pltpu.VMEM)
    bf = jnp.bfloat16
    dma = pltpu.SemaphoreType.DMA
    h, gw = pl.pallas_call(
        functools.partial(kernel, dp, n, chunks),
        out_shape=(jax.ShapeDtypeStruct((length, heads), bf), jax.ShapeDtypeStruct((heads, width), bf)),
        in_specs=[any_] * 3,
        out_specs=(vmem, vmem),
        scratch_shapes=[
            pltpu.VMEM((chunks, length, F), bf),
            pltpu.VMEM((n, tokens, heads), bf),
            pltpu.VMEM((heads, length), bf),
            pltpu.VMEM((heads, width), bf),
            pltpu.VMEM((length, heads), jnp.float32),
            pltpu.VMEM((dp, chunks, heads, F), bf),
            pltpu.VMEM((B, 2, CORES, tokens, heads), bf),
            dma((chunks,)), dma((chunks, A)), dma((chunks, B)), dma((chunks,)), dma((chunks, B)), dma((chunks, B)),
            dma((chunks,)), dma, dma, dma, dma((B,)), dma((chunks,)), dma((chunks,)),
            dma((chunks,)), dma, dma,
        ],
        compiler_params=pltpu.CompilerParams(
            collective_id=0, has_side_effects=True, vmem_limit_bytes=limit),
    )(*[pltpu.with_memory_space_constraint(v, pltpu.HBM) for v in (g, x, w_out)])
    h, gw = pl.pallas_call(
        store,
        out_shape=(jax.ShapeDtypeStruct((length, heads), bf), jax.ShapeDtypeStruct((heads, width), bf)),
        in_specs=[any_] * 2,
        out_specs=(any_, any_),
        scratch_shapes=[dma((2,))],
        compiler_params=pltpu.CompilerParams(vmem_limit_bytes=8 * 2**20),
    )(h, gw)
    return h[None], gw


def solution(mesh):
    dp, n = mesh.shape["dp"], mesh.shape["context"]
    in_specs = (P("dp", "context", None), P("dp", "context", None), P("context", None))
    out_specs = (P("dp", None, "context"), P("context", None))
    return jax.shard_map(functools.partial(local, dp, n), mesh=mesh, in_specs=in_specs, out_specs=out_specs,
                         check_vma=False)
```
